1024 devices in a mesh: row: 32 (over y_lo, z, core), col: 32 (over x, y_hi).
Axes of the slice: x: 8, y: 8 (y_hi: 4, y_lo: 2; y = y_hi * 2 + y_lo), z: 8, core: 2. Of those that a mesh axis runs over, the one named last changes fastest.
Arguments:
- tiles: bfloat16 [32, 32, 6, 256, 256], P('row', 'col'), may hold values from -0.25 to 0.25
- tile_rows: int32 [32, 32, 6], P('row', 'col'), may hold values from 0 to 63, as said below
- tile_cols: int32 [32, 32, 6], P('row', 'col'), may hold values from 0 to 63, as said below
- tile_counts: int32 [32, 32], P('row', 'col'), may hold values from 1 to 6, as said below
- trial: float32 [2048, 16, 256], P(('row', 'col'))
- search: float32 [2048, 16, 256], P(('row', 'col'))
Outputs:
- residual: float32 [2048, 16, 256], P(('row', 'col'))
- rayleigh: float32 [16, 16], replicated
- gram: float32 [32, 32], replicated
The draws below stay inside these ranges and needn't reach their ends.
Inputs may be any that keep to these rules, and one draw needn't show every extreme that they name: `tile_rows`: every slot lies in the lower triangle: the global block row of a slot is at least its global block column. `tile_cols`: lower triangle as stated for tile_rows. `tile_counts`: some device uses all 6 slots.
All inputs are finite; a program needn't handle non-finite values.
Results may differ from the reference program's by a relative error of at most 0.0029.
Values may be sent and summed in bfloat16 or wider, within the bound.
A program may use at most 32 MiB of HBM per device.

```python
import jax
import jax.numpy as jnp
from jax import lax

STATES = 16
TILE = 256
BLK_DEV = 2
SLOTS = 6
BLOCKS = 2048
BASIS = 524288
N_ROW = 32
N_COL = 32


def slot_pairs(key):
    key = jax.random.fold_in(key, 11)
    first_key, second_key = jax.random.split(key, 2)
    shape = (N_ROW, N_COL, SLOTS)
    grid_row = jax.lax.broadcasted_iota(jnp.int32, shape, 0)
    grid_col = jax.lax.broadcasted_iota(jnp.int32, shape, 1)
    row_span = N_COL * BLK_DEV
    lowest = jnp.maximum(grid_col * BLK_DEV - grid_row * row_span, 0)
    local_rows = lowest + jax.random.randint(first_key, shape, 0, row_span - lowest)
    global_rows = grid_row * row_span + local_rows
    col_ids = jnp.arange(N_ROW * BLK_DEV, dtype=jnp.int32)
    global_cols = col_ids // BLK_DEV * N_COL * BLK_DEV + col_ids % BLK_DEV
    allowed = jnp.sum((global_cols[None, None, None, :] + grid_col[..., None] * BLK_DEV <= global_rows[..., None]).astype(jnp.int32), axis=-1)
    local_cols = jax.random.randint(second_key, shape, 0, allowed)
    return (local_rows.astype(jnp.int32), local_cols.astype(jnp.int32))


def draw_tile_rows(key, part):
    return slot_pairs(key)[0]


def draw_tile_cols(key, part):
    return slot_pairs(key)[1]


def draw_tile_counts(key, part):
    key = jax.random.fold_in(key, 5)
    first_key, second_key, third_key = jax.random.split(key, 3)
    first = jax.random.randint(first_key, (N_ROW * N_COL,), 0, SLOTS)
    second = jax.random.randint(second_key, (N_ROW * N_COL,), 0, SLOTS)
    counts = 1 + first * second // SLOTS
    fullest = jax.random.randint(third_key, (), 0, N_ROW * N_COL)
    counts = counts.at[fullest].set(SLOTS)
    return counts.reshape(N_ROW, N_COL).astype(jnp.int32)


def vector_draw(key):
    first_key, second_key = jax.random.split(key, 2)
    blocks = jnp.arange(BLOCKS, dtype=jnp.float32)
    ramp = 0.6 + 1.2 * blocks / max(BLOCKS - 1, 1)
    rough = jax.random.uniform(second_key, (BLOCKS, 1, TILE), jnp.float32, 0.5, 1.5)
    base = jax.random.normal(first_key, (BLOCKS, STATES, TILE), jnp.float32)
    return (base * ramp[:, None, None] * rough).astype(jnp.float32)


def draw_trial(key, part):
    return vector_draw(jax.random.fold_in(key, 21))


def draw_search(key, part):
    return vector_draw(jax.random.fold_in(key, 37))


def steps_of(own_key, dims, shards, low, high):
    loudness, own = 1.0, jax.random.fold_in(own_key, 6)
    for axis_at, parts in shards:
        heights = jnp.exp(jax.random.uniform(jax.random.fold_in(own, axis_at), (parts,), jnp.float32, low / len(shards), high / len(shards)))
        loudness = loudness * jnp.repeat(heights, dims[axis_at] // parts).reshape([-1 if axis == axis_at else 1 for axis in range(len(dims))])
    return loudness


def normal_values(key, shape, spread, limit, cuts=(), kind=jnp.bfloat16):
    drawn = jax.random.normal(key, shape, jnp.float32) * spread
    if len(cuts) > 0:
        drawn = steps_of(key, shape, cuts, -0.22, 0.18) * drawn
    return jnp.clip(drawn, min=-limit, max=limit).astype(kind)


def setup_inputs(seed: int = 0) -> dict:
    keys = jax.random.split(jax.random.key(seed), 7)
    tiles = normal_values(keys[0], (N_ROW, N_COL, SLOTS, TILE, TILE), (2 * TILE) ** -0.5, 0.25, ((0, 32), (1, 32)))
    tile_rows = draw_tile_rows(jax.random.fold_in(keys[6], 71), 0)
    tile_cols = draw_tile_cols(jax.random.fold_in(keys[6], 71), 0)
    tile_counts = draw_tile_counts(jax.random.fold_in(keys[6], 71), 0)
    trial = draw_trial(jax.random.fold_in(keys[6], 71), 0)
    search = draw_search(jax.random.fold_in(keys[6], 71), 0)
    return {"tiles": tiles, "tile_rows": tile_rows, "tile_cols": tile_cols, "tile_counts": tile_counts, "trial": trial, "search": search}


def inner_gram(left, right):
    return jnp.einsum('bkt,blt->kl', left, right, precision=lax.Precision.HIGHEST)

def reference(tiles, tile_rows, tile_cols, tile_counts, trial, search):
    trial_low = trial.astype(jnp.bfloat16)
    slot_ids = jnp.arange(SLOTS, dtype=jnp.int32)

    def one_device(total, flat_id):
        grid_row = flat_id // N_COL
        grid_col = flat_id % N_COL
        tile_data = tiles[grid_row, grid_col].astype(jnp.float32)
        local_rows = tile_rows[grid_row, grid_col]
        local_cols = tile_cols[grid_row, grid_col]
        global_rows = (grid_row * N_COL * BLK_DEV + local_rows).astype(jnp.int32)
        global_cols = ((local_cols // BLK_DEV * N_COL + grid_col) * BLK_DEV + local_cols % BLK_DEV).astype(jnp.int32)
        live_slots = (slot_ids < tile_counts[grid_row, grid_col]).astype(jnp.float32)[:, None, None]
        col_sel = trial_low[global_cols].astype(jnp.float32)
        row_sel = trial_low[global_rows].astype(jnp.float32)
        by_row = jnp.einsum('sij,skj->ski', tile_data, col_sel) * live_slots
        by_col = jnp.einsum('sij,ski->skj', tile_data, row_sel) * live_slots
        total = total.at[global_rows].add(by_row)
        total = total.at[global_cols].add(by_col)
        return (total, None)
    start = jnp.zeros((BLOCKS, STATES, TILE), jnp.float32)
    image, _ = lax.scan(one_device, start, jnp.arange(N_ROW * N_COL, dtype=jnp.int32))
    correlation = inner_gram(trial, trial) / BASIS
    projected = inner_gram(trial, image) / BASIS
    factor = jnp.linalg.cholesky(correlation)
    rayleigh = jax.scipy.linalg.cho_solve((factor, True), projected)
    residual = image - jnp.einsum('bkt,kl->blt', trial, rayleigh, precision=lax.Precision.HIGHEST)
    res_res = inner_gram(residual, residual) / BASIS
    res_search = inner_gram(residual, search) / BASIS
    search_search = inner_gram(search, search) / BASIS
    upper = jnp.concatenate([res_res, res_search], axis=1)
    lower = jnp.concatenate([res_search.T, search_search], axis=1)
    gram = jnp.concatenate([upper, lower], axis=0)
    return (residual, rayleigh, gram)
```

```python
import jax
import jax.numpy as jnp
from jax import lax
from jax.experimental import pallas as pl
from jax.experimental.pallas import tpu as pltpu
from jax.sharding import PartitionSpec as P

MESH = pl.DeviceIdType.MESH
HI = lax.Precision.HIGHEST
F32 = jnp.float32
BF16 = jnp.bfloat16
SLOTS = 6
STATES = 16
TILE = 256
NT = (((1,), (1,)), ((), ()))
NN = (((1,), (0,)), ((), ()))


class Sems:
    def __init__(self, send, recv):
        self.send, self.recv, self.used, self.copies = send, recv, 0, []

    def copy(self, src, dst, peer):
        at = self.used
        self.used += 1
        c = pltpu.make_async_remote_copy(
            src_ref=src, dst_ref=dst, send_sem=self.send.at[at], recv_sem=self.recv.at[at],
            device_id=peer, device_id_type=MESH)
        c.start()
        self.copies.append(c)
        return c


class Ring:
    def __init__(self, sems, at, peer, far_up):
        self.sems, self.at, self.peer, self.far_up = sems, at, peer, far_up

    def first(self):
        own = self.at(0)
        self.c = {d: self.sems.copy(own, own, self.peer(d)) for d in (2, -2, 1, -1)}

    def second(self):
        for sign in (1, -1):
            self.c[2 * sign].wait_recv()
            src = self.at(-2 * sign)
            if (sign > 0) == self.far_up:
                self.c[4] = self.sems.copy(src, src, self.peer(2 * sign))
            self.c[3 * sign] = self.sems.copy(src, src, self.peer(sign))

    def last(self):
        for d in (1, -1, 3, -3, 4):
            self.c[d].wait_recv()


def kernel(tiles, rows, cols, count, trial, search, residual, rayleigh, gram,
           tile_buf, gath_r, gath_c, con_r, con_c, code_r, code_c, acc_r, acc_c, part_r, part_c,
           ar1x, ar1h, ar1l, ar1z, ar2x, ar2h, ar2l, ar2z, pack, tile_sem, send, recv):
    p, q = lax.axis_index("row"), lax.axis_index("col")
    x, yh = q // 4, q % 4
    yl, z, core = p // 16, (p // 2) % 8, p % 2
    al = yl * 2 + core
    sems = Sems(send, recv)

    def x_peer(d):
        return (p, ((x + d + 8) % 8) * 4 + yh)

    def h_peer(d):
        return (p, x * 4 + (yh + d) % 4)

    def z_peer(d):
        return (yl * 16 + ((z + d + 8) % 8) * 2 + core, q)

    def l_peer(d):
        a = (al + d) % 4
        return ((a // 2) * 16 + z * 2 + a % 2, q)

    fetch = pltpu.make_async_copy(tiles.at[0, 0], tile_buf, tile_sem)
    fetch.start()

    barrier = pltpu.get_barrier_semaphore()
    for d in range(1, 8):
        for peer in (x_peer(d), z_peer(d)):
            pl.semaphore_signal(barrier, inc=1, device_id=peer, device_id_type=MESH)
    for d in range(1, 4):
        for peer in (h_peer(d), l_peer(d)):
            pl.semaphore_signal(barrier, inc=1, device_id=peer, device_id_type=MESH)

    used = count[0, 0]
    row_at, col_at, live = [], [], []
    for s in range(SLOTS):
        i, j = rows[0, 0, s], cols[0, 0, s]
        row_at.append(i)
        col_at.append(((j // 4) % 8) * 8 + (j // 32) * 4 + j % 4)
        live.append(jnp.where(s < used, 1.0, 0.0).astype(F32))

    low = trial[...].astype(BF16)
    own_r = pl.ds(pl.multiple_of(x * 8 + yh * 2, 2), 2)
    own_c = pl.ds(pl.multiple_of(z * 8 + al * 2, 2), 2)
    gath_r[own_r] = low
    gath_c[own_c] = low

    lane = lax.broadcasted_iota(jnp.int32, (8, 128), 1)
    for at, code, me in ((row_at, code_r, x), (col_at, code_c, z)):
        value = jnp.full((8, 128), -1.0, F32)
        for s in range(SLOTS):
            target = (at[s] * 16 + lane % 16).astype(F32)
            value = jnp.where(lane // 16 == s, target * live[s] - (1.0 - live[s]), value)
        code[me] = value
    pad = jnp.zeros((8, 32, TILE), BF16)
    con_r[:, 96:, :] = pad
    con_c[:, 96:, :] = pad
    pack[...] = jnp.zeros(pack.shape, F32)

    trial_cat = jnp.concatenate([trial[0], trial[1]], axis=1)
    search_cat = jnp.concatenate([search[0], search[1]], axis=1)
    corr = lax.dot_general(trial_cat, trial_cat, NT, precision=HI, preferred_element_type=F32)

    pl.semaphore_wait(barrier, 20)

    def ring_of(buf, base, me_b, me_a, peer, d):
        def at(off):
            return buf.at[pl.ds(((me_b + off + 8) % 8) * 8 + ((me_a - d + 4) % 4) * 2, 2)]
        return Ring(sems, at, peer, d < 2)

    rings_r = [ring_of(gath_r, 0, x, yh, x_peer, d) for d in range(4)]
    rings_c = [ring_of(gath_c, 0, z, al, z_peer, d) for d in range(4)]
    group_c = {d: sems.copy(gath_c.at[own_c], gath_c.at[own_c], l_peer(d)) for d in (1, 2, 3)}
    group_r = {d: sems.copy(gath_r.at[own_r], gath_r.at[own_r], h_peer(d)) for d in (2, 1, 3)}
    rings_r[0].first()
    rings_c[0].first()
    for d in (1, 2, 3):
        group_c[d].wait_recv()
        rings_c[d].first()
    for d in (1, 3):
        group_r[d].wait_recv()
        rings_r[d].first()
    rings_r[0].second()
    rings_c[0].second()
    group_r[2].wait_recv()
    rings_r[2].first()
    for d in (1, 3, 2):
        rings_c[d].second()
        rings_r[d].second()
    codes = []
    for d in range(1, 8):
        codes.append(sems.copy(code_r.at[x], code_r.at[x], x_peer(d)))
        codes.append(sems.copy(code_c.at[z], code_c.at[z], z_peer(d)))
    fetch.wait()
    for d in (0, 1, 3, 2):
        rings_c[d].last()
        rings_r[d].last()

    def con_ring(buf, me, peer, half):
        def at(off):
            return buf.at[(me + off + 8) % 8, pl.ds(half * 48, 48)]
        return Ring(sems, at, peer, half == 0)

    out_r = [con_ring(con_r, x, x_peer, h) for h in range(2)]
    out_c = [con_ring(con_c, z, z_peer, h) for h in range(2)]
    row_sel = [gath_r[row_at[s]] for s in range(SLOTS)]
    by_row = []
    for s in range(SLOTS):
        col_sel = gath_c[col_at[s]]
        product = lax.dot_general(col_sel, tile_buf[s], NT, preferred_element_type=F32) * live[s]
        by_row.append(product)
        con_r[x, pl.ds(s * 16, 16), :] = product.astype(BF16)

    def group_start(buf, me, peer, value, n):
        buf[me] = value
        own = buf.at[me]
        return [sems.copy(own, own, peer(d)) for d in range(1, n)]

    def group_sum(buf, copies, n):
        for c in copies:
            c.wait_recv()
        total = buf[0]
        for i in range(1, n):
            total = total + buf[i]
        return total

    left = jnp.concatenate([v.astype(F32) for v in row_sel], axis=1)
    right = jnp.concatenate(by_row, axis=1)
    mixed = lax.dot_general(left, right, NT, precision=HI, preferred_element_type=F32)
    pack[0:16, 0:16] = corr
    pack[16:32, 0:16] = mixed
    both = (pack[0:8] + pltpu.roll(pack[8:16], 32, 1) + pltpu.roll(pack[16:24], 64, 1)
            + pltpu.roll(pack[24:32], 96, 1))
    first_x = group_start(ar1x, x, x_peer, both, 8)
    out_r[0].first()
    out_r[1].first()

    for s in range(SLOTS):
        product = lax.dot_general(row_sel[s], tile_buf[s], NN, preferred_element_type=F32) * live[s]
        con_c[z, pl.ds(s * 16, 16), :] = product.astype(BF16)
    out_c[0].first()
    out_c[1].first()

    first_h = group_start(ar1h, yh, h_peer, group_sum(ar1x, first_x, 8), 4)
    for ring in (out_r[0], out_c[0], out_r[1], out_c[1]):
        ring.second()
    first_l = group_start(ar1l, al, l_peer, group_sum(ar1h, first_h, 4), 4)
    first_z = group_start(ar1z, z, z_peer, group_sum(ar1l, first_l, 4), 8)

    for c in codes:
        c.wait_recv()
    sub = lax.broadcasted_iota(jnp.int32, (128, 128), 0)

    def reduce_first(buf, code, rings, me_b, me_a, acc, part, peer):
        for ring in rings:
            ring.last()
        base = (sub + me_b * 128).astype(F32)
        total = jnp.zeros((128, TILE), F32)
        for b in range(8):
            pick = jnp.where(code[b][0:1, :] == base, 1.0, 0.0).astype(BF16)
            total = total + lax.dot_general(pick, buf[b], NN, preferred_element_type=F32)
        acc[...] = total.reshape(4, 32, TILE)
        return [sems.copy(acc.at[(me_a + d) % 4], part.at[d - 1], peer(d)) for d in (2, 1, 3)]

    parts = reduce_first(con_r, code_r, out_r, x, yh, acc_r, part_r, h_peer)
    parts = parts + reduce_first(con_c, code_c, out_c, z, al, acc_c, part_c, l_peer)

    total = group_sum(ar1z, first_z, 8) / BASIS
    corr = jnp.concatenate([total, pltpu.roll(total, 96, 1)], axis=0)
    mixed = jnp.concatenate([pltpu.roll(total, 64, 1), pltpu.roll(total, 32, 1)], axis=0)
    ident = (lax.broadcasted_iota(jnp.int32, (16, 16), 0)
             == lax.broadcasted_iota(jnp.int32, (16, 16), 1)).astype(F32)
    flip = lax.dot_general(ident, mixed[:, 0:16], NT, precision=HI, preferred_element_type=F32)
    pack[0:16, 0:16] = corr[:, 0:16]
    pack[0:16, 16:32] = mixed[:, 0:16] + flip
    work = pack[0:16, :]
    row_id = lax.broadcasted_iota(jnp.int32, (16, 128), 0)
    for j in range(STATES):
        pivot = work[j:j + 1, :] / work[j:j + 1, j:j + 1]
        work = jnp.where(row_id == j, pivot, work - work[:, j:j + 1] * pivot)
    pack[0:16, :] = work
    quotient = pack[0:16, 16:32]
    rayleigh[...] = quotient
    turned = lax.dot_general(ident, quotient, NT, precision=HI, preferred_element_type=F32)

    for c in parts:
        c.wait_recv()
    image = (acc_r[yh] + part_r[0] + part_r[1] + part_r[2]
             + acc_c[al] + part_c[0] + part_c[1] + part_c[2])
    fixed = lax.dot_general(turned, trial_cat, NN, precision=HI, preferred_element_type=F32)
    res0 = image[0:16] - fixed[:, 0:TILE]
    res1 = image[16:32] - fixed[:, TILE:]
    residual[0] = res0
    residual[1] = res1
    stack = jnp.concatenate([jnp.concatenate([res0, res1], axis=1), search_cat], axis=0)
    local = lax.dot_general(stack, stack, NT, precision=HI, preferred_element_type=F32)
    pack[...] = jnp.zeros(pack.shape, F32)
    pack[:, 0:32] = local
    both = (pack[0:8] + pltpu.roll(pack[8:16], 32, 1) + pltpu.roll(pack[16:24], 64, 1)
            + pltpu.roll(pack[24:32], 96, 1))
    step = group_start(ar2x, x, x_peer, both, 8)
    step = group_start(ar2h, yh, h_peer, group_sum(ar2x, step, 8), 4)
    step = group_start(ar2l, al, l_peer, group_sum(ar2h, step, 4), 4)
    step = group_start(ar2z, z, z_peer, group_sum(ar2l, step, 4), 8)
    total = group_sum(ar2z, step, 8) / BASIS
    for g in range(4):
        spread = total if g == 0 else pltpu.roll(total, 128 - 32 * g, 1)
        gram[8 * g:8 * g + 8, :] = spread[:, 0:32]

    for c in sems.copies:
        c.wait_send()


BASIS = 524288.0
COPIES = 150


def local(tiles, tile_rows, tile_cols, tile_counts, trial, search):
    smem = pl.BlockSpec(memory_space=pltpu.SMEM)
    vmem = pl.BlockSpec(memory_space=pltpu.VMEM)
    return pl.pallas_call(
        kernel,
        out_shape=(
            jax.ShapeDtypeStruct((2, STATES, TILE), F32),
            jax.ShapeDtypeStruct((STATES, STATES), F32),
            jax.ShapeDtypeStruct((2 * STATES, 2 * STATES), F32),
        ),
        in_specs=[pl.BlockSpec(memory_space=pl.ANY), smem, smem, smem, vmem, vmem],
        out_specs=(vmem, vmem, vmem),
        scratch_shapes=[
            pltpu.VMEM((SLOTS, TILE, TILE), BF16),
            pltpu.VMEM((64, STATES, TILE), BF16),
            pltpu.VMEM((64, STATES, TILE), BF16),
            pltpu.VMEM((8, 128, TILE), BF16),
            pltpu.VMEM((8, 128, TILE), BF16),
            pltpu.VMEM((8, 8, 128), F32),
            pltpu.VMEM((8, 8, 128), F32),
            pltpu.VMEM((4, 32, TILE), F32),
            pltpu.VMEM((4, 32, TILE), F32),
            pltpu.VMEM((3, 32, TILE), F32),
            pltpu.VMEM((3, 32, TILE), F32),
        ] + [pltpu.VMEM((n, 8, 128), F32) for n in (8, 4, 4, 8, 8, 4, 4, 8)] + [
            pltpu.VMEM((32, 128), F32),
            pltpu.SemaphoreType.DMA,
            pltpu.SemaphoreType.DMA((COPIES,)),
            pltpu.SemaphoreType.DMA((COPIES,)),
        ],
        compiler_params=pltpu.CompilerParams(collective_id=0, has_side_effects=True),
    )(tiles, tile_rows, tile_cols, tile_counts, trial, search)


def solution(mesh):
    return jax.shard_map(
        local,
        mesh=mesh,
        in_specs=(
            P("row", "col", None, None, None),
            P("row", "col", None),
            P("row", "col", None),
            P("row", "col"),
            P(("row", "col"), None, None),
            P(("row", "col"), None, None),
        ),
        out_specs=(P(("row", "col"), None, None), P(), P()),
        check_vma=False,
    )
```

```python
import jax
import jax.numpy as jnp
from jax import lax
from jax.experimental import pallas as pl
from jax.experimental.pallas import tpu as pltpu
from jax.sharding import PartitionSpec as P

MESH = pl.DeviceIdType.MESH
HI = lax.Precision.HIGHEST
F32 = jnp.float32
BF16 = jnp.bfloat16
SLOTS = 6
STATES = 16
TILE = 256
NT = (((1,), (1,)), ((), ()))
NN = (((1,), (0,)), ((), ()))


class Sems:
    def __init__(self, send, recv):
        self.send, self.recv, self.used, self.copies = send, recv, 0, []

    def copy(self, src, dst, peer):
        at = self.used
        self.used += 1
        c = pltpu.make_async_remote_copy(
            src_ref=src, dst_ref=dst, send_sem=self.send.at[at], recv_sem=self.recv.at[at],
            device_id=peer, device_id_type=MESH)
        c.start()
        self.copies.append(c)
        return c


class Ring:
    def __init__(self, sems, at, peer, far_up):
        self.sems, self.at, self.peer, self.far_up = sems, at, peer, far_up

    def first(self):
        own = self.at(0)
        self.c = {d: self.sems.copy(own, own, self.peer(d)) for d in (2, -2, 1, -1)}

    def second(self):
        for sign in (1, -1):
            self.c[2 * sign].wait_recv()
            src = self.at(-2 * sign)
            if (sign > 0) == self.far_up:
                self.c[4] = self.sems.copy(src, src, self.peer(2 * sign))
            self.c[3 * sign] = self.sems.copy(src, src, self.peer(sign))

    def last(self):
        for d in (1, -1, 3, -3, 4):
            self.c[d].wait_recv()


class Direct(Ring):
    def first(self):
        own = self.at(0)
        self.c = {d: self.sems.copy(own, own, self.peer(d)) for d in (4, 3, -3, 2, -2, 1, -1)}

    def second(self):
        pass

    def last(self):
        for d in (1, -1, 2, -2, 3, -3, 4):
            self.c[d].wait_recv()


def pack_rows(buf, rows, shift):
    total = buf[0:8]
    for i in range(1, rows // 8):
        total = total + pltpu.roll(buf[8 * i:8 * i + 8], shift * i, 1)
    return total


def kernel(tiles, rows, cols, count, trial, search, residual, rayleigh, gram,
           tile_buf, gath_r, gath_c, con_r, con_c, code_r, code_c, acc_r, acc_c, low_r, low_c, part_r, part_c,
           ar0x, ar0y, ar0z, ar1x, ar1y, ar1z, pack, known, tile_sem, send, recv):
    p, q = lax.axis_index("row"), lax.axis_index("col")
    x, yh = q // 4, q % 4
    yl, z, core = p // 16, (p // 2) % 8, p % 2
    al = yl * 2 + core
    yc = (yh * 2 + yl) * 2 + core
    sems = Sems(send, recv)

    def x_peer(d):
        return (p, ((x + d + 8) % 8) * 4 + yh)

    def h_peer(d):
        return (p, x * 4 + (yh + d) % 4)

    def z_peer(d):
        return (yl * 16 + ((z + d + 8) % 8) * 2 + core, q)

    def l_peer(d):
        a = (al + d) % 4
        return ((a // 2) * 16 + z * 2 + a % 2, q)

    def y_peer(d):
        a = (yc + d) % 16
        return (((a // 2) % 2) * 16 + z * 2 + a % 2, x * 4 + a // 4)

    ring_order = (4, 3, 5, 2, 6, 1, 7)
    y_order = (8, 9, 7, 6, 10, 11, 5, 4, 12, 13, 3, 2, 14, 15, 1)

    barrier = pltpu.get_barrier_semaphore()
    for peer in [x_peer(d) for d in ring_order] + [z_peer(d) for d in ring_order] + [y_peer(d) for d in y_order]:
        pl.semaphore_signal(barrier, inc=1, device_id=peer, device_id_type=MESH)
    fetch = pltpu.make_async_copy(tiles.at[0, 0], tile_buf, tile_sem)
    fetch.start()

    low = trial[...].astype(BF16)
    own_r = pl.ds(pl.multiple_of(x * 8 + yh * 2, 2), 2)
    own_c = pl.ds(pl.multiple_of(z * 8 + al * 2, 2), 2)
    gath_r[own_r] = low
    gath_c[own_c] = low

    trial_cat = jnp.concatenate([trial[0], trial[1]], axis=1)
    search_cat = jnp.concatenate([search[0], search[1]], axis=1)
    held = jnp.concatenate([trial_cat, search_cat], axis=0)
    pack[...] = jnp.zeros(pack.shape, F32)
    pack[:, 0:32] = lax.dot_general(held, held, NT, precision=HI, preferred_element_type=F32)

    pl.semaphore_wait(barrier, 29)

    def group_start(buf, me, peer, order, value):
        buf[me] = value
        own = buf.at[me]
        return [sems.copy(own, own, peer(d)) for d in order]

    def group_sum(buf, copies, n):
        for c in copies:
            c.wait_recv()
        total = buf[0]
        for i in range(1, n):
            total = total + buf[i]
        return total

    def ring_of(kind, buf, me_b, me_a, peer, d):
        def at(off):
            return buf.at[pl.ds(((me_b + off + 8) % 8) * 8 + ((me_a - d + 4) % 4) * 2, 2)]
        return kind(sems, at, peer, d < 2)

    rings_r = [ring_of(Direct if d == 2 else Ring, gath_r, x, yh, x_peer, d) for d in range(4)]
    rings_c = [ring_of(Ring, gath_c, z, al, z_peer, d) for d in range(4)]
    group_r = {d: sems.copy(gath_r.at[own_r], gath_r.at[own_r], h_peer(d)) for d in (2, 1, 3)}
    rings_r[0].first()
    group_c = {d: sems.copy(gath_c.at[own_c], gath_c.at[own_c], l_peer(d)) for d in (2, 1, 3)}
    rings_c[0].first()

    used = count[...]
    row_at, col_at, live = [], [], []
    for s in range(SLOTS):
        i, j = rows[0, 0, s], cols[0, 0, s]
        row_at.append(i)
        col_at.append(((j // 4) % 8) * 8 + (j // 32) * 4 + j % 4)
        live.append(jnp.where(s < used, 1.0, 0.0).astype(F32))
    lane = lax.broadcasted_iota(jnp.int32, (8, 128), 1)
    for at, code, me in ((row_at, code_r, x), (col_at, code_c, z)):
        value = jnp.full((8, 128), -1.0, F32)
        for s in range(SLOTS):
            target = (at[s] * 16 + lane % 16).astype(F32)
            value = jnp.where(lane // 16 == s, target * live[s] - (1.0 - live[s]), value)
        code[me] = value

    codes = []
    for d in ring_order:
        codes.append(sems.copy(code_r.at[x], code_r.at[x], x_peer(d)))
        codes.append(sems.copy(code_c.at[z], code_c.at[z], z_peer(d)))

    for d in (1, 2, 3):
        group_c[d].wait_recv()
        rings_c[d].first()
    ar0 = group_start(ar0x, x, x_peer, ring_order, pack_rows(pack, 32, 32))
    for d in (1, 3):
        group_r[d].wait_recv()
        rings_r[d].first()
    rings_r[0].second()
    rings_c[0].second()
    group_r[2].wait_recv()
    rings_r[2].first()
    for d in (1, 2, 3):
        rings_c[d].second()
    for d in (1, 3):
        rings_r[d].second()
    ar0 = group_start(ar0y, yc, y_peer, y_order, group_sum(ar0x, ar0, 8))
    pad = jnp.zeros((8, 32, TILE), BF16)
    con_r[:, 96:, :] = pad
    con_c[:, 96:, :] = pad
    fetch.wait()
    for d in (0, 1, 2, 3):
        rings_c[d].last()
    for d in (0, 1, 3, 2):
        rings_r[d].last()

    def con_ring(buf, me, peer, half):
        def at(off):
            return buf.at[(me + off + 8) % 8, pl.ds(half * 48, 48)]
        return Ring(sems, at, peer, half == 0)

    out_r = [con_ring(con_r, x, x_peer, h) for h in range(2)]
    out_c = [con_ring(con_c, z, z_peer, h) for h in range(2)]
    for s in range(SLOTS):
        product = lax.dot_general(gath_c[col_at[s]], tile_buf[s], NT, preferred_element_type=F32) * live[s]
        con_r[x, pl.ds(s * 16, 16), :] = product.astype(BF16)
        if s % 3 == 2:
            out_r[s // 3].first()
    for s in range(SLOTS):
        product = lax.dot_general(gath_r[row_at[s]], tile_buf[s], NN, preferred_element_type=F32) * live[s]
        con_c[z, pl.ds(s * 16, 16), :] = product.astype(BF16)
        if s % 3 == 2:
            out_c[s // 3].first()
    for ring in (out_r[0], out_r[1], out_c[0], out_c[1]):
        ring.second()
    ar0 = group_start(ar0z, z, z_peer, ring_order, group_sum(ar0y, ar0, 16))
    for c in codes:
        c.wait_recv()

    sub = lax.broadcasted_iota(jnp.int32, (128, 128), 0)

    def reduce_first(buf, code, rings, me_b, me_a, acc, low, part, peer):
        base = (sub + me_b * 128).astype(F32)
        picks = [jnp.where(code[b][0:1, :] == base, 1.0, 0.0).astype(BF16) for b in range(8)]
        for ring in rings:
            ring.last()
        total = jnp.zeros((128, TILE), F32)
        for b in range(0, 8, 2):
            pick = jnp.concatenate(picks[b:b + 2], axis=1)
            total = total + lax.dot_general(
                pick, buf[b:b + 2].reshape(256, TILE), NN, preferred_element_type=F32)
        acc[...] = total.reshape(4, 32, TILE)
        low[...] = total.astype(BF16).reshape(4, 32, TILE)
        return [sems.copy(low.at[(me_a + d) % 4], part.at[d - 1], peer(d)) for d in (2, 1, 3)]

    parts = reduce_first(con_r, code_r, out_r, x, yh, acc_r, low_r, part_r, h_peer)
    parts = parts + reduce_first(con_c, code_c, out_c, z, al, acc_c, low_c, part_c, l_peer)

    total = group_sum(ar0z, ar0, 8) / BASIS
    known[0:16] = jnp.concatenate([total, pltpu.roll(total, 96, 1)], axis=0)
    known[16:32] = jnp.concatenate([pltpu.roll(total, 64, 1), pltpu.roll(total, 32, 1)], axis=0)
    row_id = lax.broadcasted_iota(jnp.int32, (16, 128), 0)
    lane_id = lax.broadcasted_iota(jnp.int32, (16, 128), 1)
    ident = jnp.where(lane_id == row_id, 1.0, 0.0).astype(F32)
    work = jnp.where(lane_id < 16, known[0:16], pltpu.roll(ident, 16, 1))
    for j in range(STATES):
        pivot = work[j:j + 1, :] / work[j:j + 1, j:j + 1]
        work = jnp.where(row_id == j, pivot, work - work[:, j:j + 1] * pivot)
    pack[0:16, :] = work
    inverse = pack[0:16, 16:32]
    gram[16:32, 16:32] = known[16:32, 16:32]
    pack[...] = jnp.zeros(pack.shape, F32)
    for c in parts:
        c.wait_recv()
    image = acc_r[yh] + acc_c[al]
    for i in range(3):
        image = image + part_r[i].astype(F32) + part_c[i].astype(F32)
    image_cat = jnp.concatenate([image[0:16], image[16:32]], axis=1)
    stack = jnp.concatenate([trial_cat, image_cat, search_cat], axis=0)
    pack[0:16, 0:48] = lax.dot_general(image_cat, stack, NT, precision=HI, preferred_element_type=F32)
    step = group_start(ar1x, x, x_peer, ring_order, pack_rows(pack, 16, 64))

    step = group_start(ar1y, yc, y_peer, y_order, group_sum(ar1x, step, 8))
    step = group_start(ar1z, z, z_peer, ring_order, group_sum(ar1y, step, 16))
    total = group_sum(ar1z, step, 8) / BASIS

    pack[0:16, :] = jnp.concatenate([total, pltpu.roll(total, 64, 1)], axis=0)
    mixed = pack[0:16, 0:16]
    turned = lax.dot_general(mixed, inverse, NN, precision=HI, preferred_element_type=F32)
    fixed = lax.dot_general(turned, trial_cat, NN, precision=HI, preferred_element_type=F32)
    residual[0] = image[0:16] - fixed[:, 0:TILE]
    residual[1] = image[16:32] - fixed[:, TILE:]
    rayleigh[...] = lax.dot_general(inverse, mixed, NT, precision=HI, preferred_element_type=F32)
    gram[0:16, 0:16] = pack[0:16, 16:32] - lax.dot_general(
        turned, mixed, NT, precision=HI, preferred_element_type=F32)
    side = pack[0:16, 32:48] - lax.dot_general(
        turned, known[0:16, 16:32], NN, precision=HI, preferred_element_type=F32)
    gram[0:16, 16:32] = side
    gram[16:32, 0:16] = lax.dot_general(
        ident[:, 0:16], side, NT, precision=HI, preferred_element_type=F32)

    for c in sems.copies:
        c.wait_send()


def hand_on(a, b, c, a_out, b_out, c_out):
    a_out[...] = a[...]
    b_out[...] = b[...]
    c_out[...] = c[...]


BASIS = 524288.0
COPIES = 168


def local(tiles, tile_rows, tile_cols, tile_counts, trial, search):
    smem = pl.BlockSpec(memory_space=pltpu.SMEM)
    vmem = pl.BlockSpec(memory_space=pltpu.VMEM)
    results = pl.pallas_call(
        kernel,
        out_shape=(
            jax.ShapeDtypeStruct((2, STATES, TILE), F32),
            jax.ShapeDtypeStruct((STATES, STATES), F32),
            jax.ShapeDtypeStruct((2 * STATES, 2 * STATES), F32),
        ),
        in_specs=[pl.BlockSpec(memory_space=pl.ANY), smem, smem, vmem, vmem, vmem],
        out_specs=(vmem, vmem, vmem),
        scratch_shapes=[
            pltpu.VMEM((SLOTS, TILE, TILE), BF16),
            pltpu.VMEM((64, STATES, TILE), BF16),
            pltpu.VMEM((64, STATES, TILE), BF16),
            pltpu.VMEM((8, 128, TILE), BF16),
            pltpu.VMEM((8, 128, TILE), BF16),
            pltpu.VMEM((8, 8, 128), F32),
            pltpu.VMEM((8, 8, 128), F32),
            pltpu.VMEM((4, 32, TILE), F32),
            pltpu.VMEM((4, 32, TILE), F32),
            pltpu.VMEM((4, 32, TILE), BF16),
            pltpu.VMEM((4, 32, TILE), BF16),
            pltpu.VMEM((3, 32, TILE), BF16),
            pltpu.VMEM((3, 32, TILE), BF16),
        ] + [pltpu.VMEM((n, 8, 128), F32) for n in (8, 16, 8, 8, 16, 8)] + [
            pltpu.VMEM((32, 128), F32),
            pltpu.VMEM((32, 128), F32),
            pltpu.SemaphoreType.DMA,
            pltpu.SemaphoreType.DMA((COPIES,)),
            pltpu.SemaphoreType.DMA((COPIES,)),
        ],
        compiler_params=pltpu.CompilerParams(collective_id=0, has_side_effects=True),
    )(tiles, tile_rows, tile_cols, tile_counts, trial, search)
    return pl.pallas_call(
        hand_on,
        out_shape=tuple(jax.ShapeDtypeStruct(r.shape, F32) for r in results),
        in_specs=[vmem] * 3,
        out_specs=(vmem,) * 3,
    )(*results)


def solution(mesh):
    return jax.shard_map(
        local,
        mesh=mesh,
        in_specs=(
            P("row", "col", None, None, None),
            P("row", "col", None),
            P("row", "col", None),
            P("row", "col"),
            P(("row", "col"), None, None),
            P(("row", "col"), None, None),
        ),
        out_specs=(P(("row", "col"), None, None), P(), P()),
        check_vma=False,
    )
```

```python
import jax
import jax.numpy as jnp
from jax import lax
from jax.experimental import pallas as pl
from jax.experimental.pallas import tpu as pltpu
from jax.sharding import PartitionSpec as P

MESH = pl.DeviceIdType.MESH
HI = lax.Precision.HIGHEST
F32 = jnp.float32
BF16 = jnp.bfloat16
SLOTS = 6
STATES = 16
TILE = 256
NT = (((1,), (1,)), ((), ()))
NN = (((1,), (0,)), ((), ()))


class Sems:
    def __init__(self, send, recv):
        self.send, self.recv, self.used, self.copies = send, recv, 0, []

    def copy(self, src, dst, peer):
        at = self.used
        self.used += 1
        c = pltpu.make_async_remote_copy(
            src_ref=src, dst_ref=dst, send_sem=self.send.at[at], recv_sem=self.recv.at[at],
            device_id=peer, device_id_type=MESH)
        c.start()
        self.copies.append(c)
        return c


class Ring:
    def __init__(self, sems, at, peer, far_up):
        self.sems, self.at, self.peer, self.far_up, self.c = sems, at, peer, far_up, {}

    def first(self, distances=(2, -2, 1, -1)):
        own = self.at(0)
        for d in distances:
            self.c[d] = self.sems.copy(own, own, self.peer(d))

    def second(self):
        for sign in (1, -1):
            self.c[2 * sign].wait_recv()
            src = self.at(-2 * sign)
            if (sign > 0) == self.far_up:
                self.c[4] = self.sems.copy(src, src, self.peer(2 * sign))
            self.c[3 * sign] = self.sems.copy(src, src, self.peer(sign))

    def last(self):
        for d in (1, -1, 3, -3, 4):
            self.c[d].wait_recv()


class Direct(Ring):
    def first(self, distances=(4, 3, -3, 2, -2, 1, -1)):
        Ring.first(self, distances)

    def second(self):
        pass

    def last(self):
        for d in (1, -1, 2, -2, 3, -3, 4):
            self.c[d].wait_recv()


def pack_rows(buf, rows, shift):
    total = buf[0:8]
    for i in range(1, rows // 8):
        total = total + pltpu.roll(buf[8 * i:8 * i + 8], shift * i, 1)
    return total


def kernel(tiles, rows, cols, count, trial, search, residual, rayleigh, gram,
           tile_buf, gath_r, gath_c, con_r, con_c, code_r, code_c, acc_r, acc_c, low_r, low_c, part_r, part_c,
           ar0x, ar0y, ar0z, ar1x, ar1y, ar1z, pack, known, tile_sem, send, recv):
    p, q = lax.axis_index("row"), lax.axis_index("col")
    x, yh = q // 4, q % 4
    yl, z, core = p // 16, (p // 2) % 8, p % 2
    al = yl * 2 + core
    yc = (yh * 2 + yl) * 2 + core
    sems = Sems(send, recv)

    def x_peer(d):
        return (p, ((x + d + 8) % 8) * 4 + yh)

    def h_peer(d):
        return (p, x * 4 + (yh + d) % 4)

    def z_peer(d):
        return (yl * 16 + ((z + d + 8) % 8) * 2 + core, q)

    def l_peer(d):
        a = (al + d) % 4
        return ((a // 2) * 16 + z * 2 + a % 2, q)

    def y_peer(d):
        a = (yc + d) % 16
        return (((a // 2) % 2) * 16 + z * 2 + a % 2, x * 4 + a // 4)

    ring_order = (4, 3, 5, 2, 6, 1, 7)
    y_order = (8, 9, 7, 6, 10, 11, 5, 4, 12, 13, 3, 2, 14, 15, 1)

    barrier = pltpu.get_barrier_semaphore()
    for peer in [x_peer(d) for d in ring_order] + [z_peer(d) for d in ring_order] + [y_peer(d) for d in y_order]:
        pl.semaphore_signal(barrier, inc=1, device_id=peer, device_id_type=MESH)
    fetch = pltpu.make_async_copy(tiles.at[0, 0], tile_buf, tile_sem)
    fetch.start()

    low = trial[...].astype(BF16)
    own_r = pl.ds(pl.multiple_of(x * 8 + yh * 2, 2), 2)
    own_c = pl.ds(pl.multiple_of(z * 8 + al * 2, 2), 2)
    gath_r[own_r] = low
    gath_c[own_c] = low

    trial_cat = jnp.concatenate([trial[0], trial[1]], axis=1)
    search_cat = jnp.concatenate([search[0], search[1]], axis=1)
    held = jnp.concatenate([trial_cat, search_cat], axis=0)
    pack[...] = jnp.zeros(pack.shape, F32)
    pack[:, 0:32] = lax.dot_general(held, held, NT, precision=HI, preferred_element_type=F32)

    pl.semaphore_wait(barrier, 29)

    def group_start(buf, me, peer, order, value):
        buf[me] = value
        own = buf.at[me]
        return [sems.copy(own, own, peer(d)) for d in order]

    def group_sum(buf, copies, n):
        for c in copies:
            c.wait_recv()
        total = buf[0]
        for i in range(1, n):
            total = total + buf[i]
        return total

    def ring_of(kind, buf, me_b, me_a, peer, d):
        def at(off):
            return buf.at[pl.ds(((me_b + off + 8) % 8) * 8 + ((me_a - d + 4) % 4) * 2, 2)]
        return kind(sems, at, peer, d < 2)

    rings_r = [ring_of(Direct if d == 2 else Ring, gath_r, x, yh, x_peer, d) for d in range(4)]
    rings_c = [ring_of(Ring, gath_c, z, al, z_peer, d) for d in range(4)]
    group_r = {d: sems.copy(gath_r.at[own_r], gath_r.at[own_r], h_peer(d)) for d in (2, 1, 3)}
    rings_r[0].first()
    group_c = {d: sems.copy(gath_c.at[own_c], gath_c.at[own_c], l_peer(d)) for d in (2, 1, 3)}
    rings_c[0].first()

    used = count[...]
    row_at, col_at, live = [], [], []
    for s in range(SLOTS):
        i, j = rows[0, 0, s], cols[0, 0, s]
        row_at.append(i)
        col_at.append(((j // 4) % 8) * 8 + (j // 32) * 4 + j % 4)
        live.append(jnp.where(s < used, 1.0, 0.0).astype(F32))
    lane = lax.broadcasted_iota(jnp.int32, (8, 128), 1)
    for at, code, me in ((row_at, code_r, x), (col_at, code_c, z)):
        value = jnp.full((8, 128), -1.0, F32)
        for s in range(SLOTS):
            target = (at[s] * 16 + lane % 16).astype(F32)
            value = jnp.where(lane // 16 == s, target * live[s] - (1.0 - live[s]), value)
        code[me] = value

    codes = []
    for d in ring_order:
        codes.append(sems.copy(code_r.at[x], code_r.at[x], x_peer(d)))
        codes.append(sems.copy(code_c.at[z], code_c.at[z], z_peer(d)))

    for d in (1, 2, 3):
        group_c[d].wait_recv()
        rings_c[d].first()
    ar0 = group_start(ar0x, x, x_peer, ring_order, pack_rows(pack, 32, 32))
    for d in (1, 3):
        group_r[d].wait_recv()
        rings_r[d].first()
    rings_r[0].second()
    rings_c[0].second()
    group_r[2].wait_recv()
    rings_r[2].first()
    for d in (1, 2, 3):
        rings_c[d].second()
    for d in (1, 3):
        rings_r[d].second()
    pad = jnp.zeros((8, 32, TILE), BF16)
    con_r[:, 96:, :] = pad
    con_c[:, 96:, :] = pad
    fetch.wait()

    def con_ring(buf, me, peer, piece, far_up):
        def at(off):
            return buf.at[(me + off + 8) % 8, pl.ds(piece * 32, 32)]
        return Ring(sems, at, peer, far_up)

    out_r = [con_ring(con_r, x, x_peer, i, i != 1) for i in range(3)]
    out_c = [con_ring(con_c, z, z_peer, i, i == 1) for i in range(3)]
    for d in (0, 1, 2, 3):
        rings_c[d].last()
    for s in range(SLOTS):
        product = lax.dot_general(gath_c[col_at[s]], tile_buf[s], NT, preferred_element_type=F32) * live[s]
        con_r[x, pl.ds(s * 16, 16), :] = product.astype(BF16)
        if s % 2 == 1:
            out_r[s // 2].first((2, -2))
    for ring in out_r:
        ring.first((1, -1))
    ar0 = group_start(ar0y, yc, y_peer, y_order, group_sum(ar0x, ar0, 8))
    for d in (0, 1, 3, 2):
        rings_r[d].last()
    for s in range(SLOTS):
        product = lax.dot_general(gath_r[row_at[s]], tile_buf[s], NN, preferred_element_type=F32) * live[s]
        con_c[z, pl.ds(s * 16, 16), :] = product.astype(BF16)
        if s % 2 == 1:
            out_c[s // 2].first((2, -2))
    for ring in out_c:
        ring.first((1, -1))
    for ring in out_r + out_c:
        ring.second()
    ar0 = group_start(ar0z, z, z_peer, ring_order, group_sum(ar0y, ar0, 16))
    for c in codes:
        c.wait_recv()

    sub = lax.broadcasted_iota(jnp.int32, (128, 128), 0)

    def reduce_first(buf, code, rings, me_b, me_a, acc, low, part, peer):
        base = (sub + me_b * 128).astype(F32)
        picks = [jnp.where(code[b][0:1, :] == base, 1.0, 0.0).astype(BF16) for b in range(8)]
        for ring in rings:
            ring.last()
        total = jnp.zeros((128, TILE), F32)
        for b in range(0, 8, 2):
            pick = jnp.concatenate(picks[b:b + 2], axis=1)
            total = total + lax.dot_general(
                pick, buf[b:b + 2].reshape(256, TILE), NN, preferred_element_type=F32)
        acc[...] = total.reshape(4, 32, TILE)
        low[...] = total.astype(BF16).reshape(4, 32, TILE)
        return [sems.copy(low.at[(me_a + d) % 4], part.at[d - 1], peer(d)) for d in (2, 1, 3)]

    parts = reduce_first(con_r, code_r, out_r, x, yh, acc_r, low_r, part_r, h_peer)
    parts = parts + reduce_first(con_c, code_c, out_c, z, al, acc_c, low_c, part_c, l_peer)

    pack[...] = jnp.zeros(pack.shape, F32)
    for c in parts:
        c.wait_recv()
    image = acc_r[yh] + acc_c[al]
    for i in range(3):
        image = image + part_r[i].astype(F32) + part_c[i].astype(F32)
    image_cat = jnp.concatenate([image[0:16], image[16:32]], axis=1)
    stack = jnp.concatenate([trial_cat, image_cat, search_cat], axis=0)
    pack[0:16, 0:48] = lax.dot_general(image_cat, stack, NT, precision=HI, preferred_element_type=F32)
    step = group_start(ar1x, x, x_peer, ring_order, pack_rows(pack, 16, 64))

    total = group_sum(ar0z, ar0, 8) / BASIS
    known[0:16] = jnp.concatenate([total, pltpu.roll(total, 96, 1)], axis=0)
    known[16:32] = jnp.concatenate([pltpu.roll(total, 64, 1), pltpu.roll(total, 32, 1)], axis=0)
    row_id = lax.broadcasted_iota(jnp.int32, (16, 128), 0)
    lane_id = lax.broadcasted_iota(jnp.int32, (16, 128), 1)
    ident = jnp.where(lane_id == row_id, 1.0, 0.0).astype(F32)
    work = jnp.where(lane_id < 16, known[0:16], pltpu.roll(ident, 16, 1))
    for j in range(STATES):
        pivot = work[j:j + 1, :] / work[j:j + 1, j:j + 1]
        work = jnp.where(row_id == j, pivot, work - work[:, j:j + 1] * pivot)
    pack[0:16, :] = work
    inverse = pack[0:16, 16:32]
    solved = lax.dot_general(inverse, trial_cat, NN, precision=HI, preferred_element_type=F32)
    side_solved = lax.dot_general(
        inverse, known[0:16, 16:32], NN, precision=HI, preferred_element_type=F32)
    gram[16:32, 16:32] = known[16:32, 16:32]
    step = group_start(ar1y, yc, y_peer, y_order, group_sum(ar1x, step, 8))
    step = group_start(ar1z, z, z_peer, ring_order, group_sum(ar1y, step, 16))
    total = group_sum(ar1z, step, 8) / BASIS

    pack[0:16, :] = jnp.concatenate([total, pltpu.roll(total, 64, 1)], axis=0)
    mixed = pack[0:16, 0:16]
    turned = lax.dot_general(mixed, inverse, NN, precision=HI, preferred_element_type=F32)
    fixed = lax.dot_general(mixed, solved, NN, precision=HI, preferred_element_type=F32)
    residual[0] = image[0:16] - fixed[:, 0:TILE]
    residual[1] = image[16:32] - fixed[:, TILE:]
    rayleigh[...] = lax.dot_general(inverse, mixed, NT, precision=HI, preferred_element_type=F32)
    gram[0:16, 0:16] = pack[0:16, 16:32] - lax.dot_general(
        turned, mixed, NT, precision=HI, preferred_element_type=F32)
    side = pack[0:16, 32:48] - lax.dot_general(
        mixed, side_solved, NN, precision=HI, preferred_element_type=F32)
    gram[0:16, 16:32] = side
    gram[16:32, 0:16] = lax.dot_general(
        ident[:, 0:16], side, NT, precision=HI, preferred_element_type=F32)

    for c in sems.copies:
        c.wait_send()


def hand_on(a, b, c, a_out, b_out, c_out):
    a_out[...] = a[...]
    b_out[...] = b[...]
    c_out[...] = c[...]


BASIS = 524288.0
COPIES = 182


def local(tiles, tile_rows, tile_cols, tile_counts, trial, search):
    smem = pl.BlockSpec(memory_space=pltpu.SMEM)
    vmem = pl.BlockSpec(memory_space=pltpu.VMEM)
    results = pl.pallas_call(
        kernel,
        out_shape=(
            pltpu.VMEM((2, STATES, TILE), F32),
            pltpu.VMEM((STATES, STATES), F32),
            pltpu.VMEM((2 * STATES, 2 * STATES), F32),
        ),
        in_specs=[pl.BlockSpec(memory_space=pl.ANY), smem, smem, vmem, vmem, vmem],
        out_specs=(vmem, vmem, vmem),
        scratch_shapes=[
            pltpu.VMEM((SLOTS, TILE, TILE), BF16),
            pltpu.VMEM((64, STATES, TILE), BF16),
            pltpu.VMEM((64, STATES, TILE), BF16),
            pltpu.VMEM((8, 128, TILE), BF16),
            pltpu.VMEM((8, 128, TILE), BF16),
            pltpu.VMEM((8, 8, 128), F32),
            pltpu.VMEM((8, 8, 128), F32),
            pltpu.VMEM((4, 32, TILE), F32),
            pltpu.VMEM((4, 32, TILE), F32),
            pltpu.VMEM((4, 32, TILE), BF16),
            pltpu.VMEM((4, 32, TILE), BF16),
            pltpu.VMEM((3, 32, TILE), BF16),
            pltpu.VMEM((3, 32, TILE), BF16),
        ] + [pltpu.VMEM((n, 8, 128), F32) for n in (8, 16, 8, 8, 16, 8)] + [
            pltpu.VMEM((32, 128), F32),
            pltpu.VMEM((32, 128), F32),
            pltpu.SemaphoreType.DMA,
            pltpu.SemaphoreType.DMA((COPIES,)),
            pltpu.SemaphoreType.DMA((COPIES,)),
        ],
        compiler_params=pltpu.CompilerParams(collective_id=0, has_side_effects=True),
    )(tiles, tile_rows, tile_cols, tile_counts, trial, search)
    return pl.pallas_call(
        hand_on,
        out_shape=tuple(jax.ShapeDtypeStruct(r.shape, F32) for r in results),
        in_specs=[vmem] * 3,
        out_specs=(vmem,) * 3,
    )(*[pltpu.with_memory_space_constraint(r, pltpu.VMEM) for r in results])


def solution(mesh):
    return jax.shard_map(
        local,
        mesh=mesh,
        in_specs=(
            P("row", "col", None, None, None),
            P("row", "col", None),
            P("row", "col", None),
            P("row", "col"),
            P(("row", "col"), None, None),
            P(("row", "col"), None, None),
        ),
        out_specs=(P(("row", "col"), None, None), P(), P()),
        check_vma=False,
    )
```

```python
import jax
import jax.numpy as jnp
from jax import lax
from jax.experimental import pallas as pl
from jax.experimental.pallas import tpu as pltpu
from jax.sharding import PartitionSpec as P

MESH = pl.DeviceIdType.MESH
HI = lax.Precision.HIGHEST
F32 = jnp.float32
BF16 = jnp.bfloat16
SLOTS = 6
STATES = 16
TILE = 256
NT = (((1,), (1,)), ((), ()))
NN = (((1,), (0,)), ((), ()))


class Sems:
    def __init__(self, send, recv):
        self.send, self.recv, self.used, self.copies = send, recv, 0, []

    def copy(self, src, dst, peer):
        at = self.used
        self.used += 1
        c = pltpu.make_async_remote_copy(
            src_ref=src, dst_ref=dst, send_sem=self.send.at[at], recv_sem=self.recv.at[at],
            device_id=peer, device_id_type=MESH)
        c.start()
        self.copies.append(c)
        return c


class Ring:
    def __init__(self, sems, at, peer, far_up):
        self.sems, self.at, self.peer, self.far_up, self.c = sems, at, peer, far_up, {}

    def first(self, distances=(2, -2, 1, -1)):
        own = self.at(0)
        for d in distances:
            self.c[d] = self.sems.copy(own, own, self.peer(d))

    def second(self):
        for sign in (1, -1):
            self.c[2 * sign].wait_recv()
            src = self.at(-2 * sign)
            if (sign > 0) == self.far_up:
                self.c[4] = self.sems.copy(src, src, self.peer(2 * sign))
            self.c[3 * sign] = self.sems.copy(src, src, self.peer(sign))

    def last(self):
        for d in (1, -1, 3, -3, 4):
            self.c[d].wait_recv()


class Direct(Ring):
    def first(self, distances=(4, 3, -3, 2, -2, 1, -1)):
        Ring.first(self, distances)

    def second(self):
        pass

    def last(self):
        for d in (1, -1, 2, -2, 3, -3, 4):
            self.c[d].wait_recv()


def pack_rows(buf, rows, shift):
    total = buf[0:8]
    for i in range(1, rows // 8):
        total = total + pltpu.roll(buf[8 * i:8 * i + 8], shift * i, 1)
    return total


def kernel(tiles, rows_in, cols_in, count_in, trial_in, search_in, residual, rayleigh, gram,
           tile_buf, gath_r, gath_c, con_r, con_c, code_r, code_c, acc_r, acc_c, low_r, low_c, part_r, part_c,
           trial, search, rows, cols, count, in_sem, ar0x, ar0y, ar0z, ar1x, ar1y, ar1z, pack, known, tile_sem, send, recv):
    p, q = lax.axis_index("row"), lax.axis_index("col")
    x, yh = q // 4, q % 4
    yl, z, core = p // 16, (p // 2) % 8, p % 2
    al = yl * 2 + core
    yc = (yh * 2 + yl) * 2 + core
    sems = Sems(send, recv)

    def x_peer(d):
        return (p, ((x + d + 8) % 8) * 4 + yh)

    def h_peer(d):
        return (p, x * 4 + (yh + d) % 4)

    def z_peer(d):
        return (yl * 16 + ((z + d + 8) % 8) * 2 + core, q)

    def l_peer(d):
        a = (al + d) % 4
        return ((a // 2) * 16 + z * 2 + a % 2, q)

    def y_peer(d):
        a = (yc + d) % 16
        return (((a // 2) % 2) * 16 + z * 2 + a % 2, x * 4 + a // 4)

    ring_order = (4, 3, 5, 2, 6, 1, 7)
    y_order = (8, 9, 7, 6, 10, 11, 5, 4, 12, 13, 3, 2, 14, 15, 1)

    barrier = pltpu.get_barrier_semaphore()
    for peer in [x_peer(d) for d in ring_order] + [z_peer(d) for d in ring_order] + [y_peer(d) for d in y_order]:
        pl.semaphore_signal(barrier, inc=1, device_id=peer, device_id_type=MESH)
    loads = [pltpu.make_async_copy(src, dst, in_sem.at[i]) for i, (src, dst) in enumerate((
        (trial_in, trial), (search_in, search), (rows_in, rows), (cols_in, cols), (count_in, count)))]
    for load in loads:
        load.start()
    fetch = pltpu.make_async_copy(tiles.at[0, 0], tile_buf, tile_sem)
    fetch.start()
    loads[0].wait()

    low = trial[...].astype(BF16)
    own_r = pl.ds(pl.multiple_of(x * 8 + yh * 2, 2), 2)
    own_c = pl.ds(pl.multiple_of(z * 8 + al * 2, 2), 2)
    gath_r[own_r] = low
    gath_c[own_c] = low

    pl.semaphore_wait(barrier, 29)

    def group_start(buf, me, peer, order, value):
        buf[me] = value
        own = buf.at[me]
        return [sems.copy(own, own, peer(d)) for d in order]

    def group_sum(buf, copies, n):
        for c in copies:
            c.wait_recv()
        total = buf[0]
        for i in range(1, n):
            total = total + buf[i]
        return total

    def ring_of(kind, buf, me_b, me_a, peer, d):
        def at(off):
            return buf.at[pl.ds(((me_b + off + 8) % 8) * 8 + ((me_a - d + 4) % 4) * 2, 2)]
        return kind(sems, at, peer, d < 2)

    rings_r = [ring_of(Direct if d == 2 else Ring, gath_r, x, yh, x_peer, d) for d in range(4)]
    rings_c = [ring_of(Ring, gath_c, z, al, z_peer, d) for d in range(4)]
    group_r = {d: sems.copy(gath_r.at[own_r], gath_r.at[own_r], h_peer(d)) for d in (2, 1, 3)}
    rings_r[0].first()
    group_c = {d: sems.copy(gath_c.at[own_c], gath_c.at[own_c], l_peer(d)) for d in (2, 1, 3)}
    rings_c[0].first()

    for load in loads[1:]:
        load.wait()
    trial_cat = jnp.concatenate([trial[0], trial[1]], axis=1)
    search_cat = jnp.concatenate([search[0], search[1]], axis=1)
    held = jnp.concatenate([trial_cat, search_cat], axis=0)
    pack[...] = jnp.zeros(pack.shape, F32)
    pack[:, 0:32] = lax.dot_general(held, held, NT, precision=HI, preferred_element_type=F32)
    used = count[0, 0]
    row_at, col_at, live = [], [], []
    for s in range(SLOTS):
        i, j = rows[0, 0, s], cols[0, 0, s]
        row_at.append(i)
        col_at.append(((j // 4) % 8) * 8 + (j // 32) * 4 + j % 4)
        live.append(jnp.where(s < used, 1.0, 0.0).astype(F32))
    lane = lax.broadcasted_iota(jnp.int32, (8, 128), 1)
    for at, code, me in ((row_at, code_r, x), (col_at, code_c, z)):
        value = jnp.full((8, 128), -1.0, F32)
        for s in range(SLOTS):
            target = (at[s] * 16 + lane % 16).astype(F32)
            value = jnp.where(lane // 16 == s, target * live[s] - (1.0 - live[s]), value)
        code[me] = value

    codes = []
    for d in ring_order:
        codes.append(sems.copy(code_r.at[x], code_r.at[x], x_peer(d)))
        codes.append(sems.copy(code_c.at[z], code_c.at[z], z_peer(d)))

    for d in (1, 2, 3):
        group_c[d].wait_recv()
        rings_c[d].first()
    ar0 = group_start(ar0x, x, x_peer, ring_order, pack_rows(pack, 32, 32))
    for d in (1, 3):
        group_r[d].wait_recv()
        rings_r[d].first()
    rings_r[0].second()
    rings_c[0].second()
    group_r[2].wait_recv()
    rings_r[2].first()
    for d in (1, 2, 3):
        rings_c[d].second()
    for d in (1, 3):
        rings_r[d].second()
    pad = jnp.zeros((8, 32, TILE), BF16)
    con_r[:, 96:, :] = pad
    con_c[:, 96:, :] = pad
    fetch.wait()

    def con_ring(buf, me, peer, piece, far_up):
        def at(off):
            return buf.at[(me + off + 8) % 8, pl.ds(piece * 32, 32)]
        return Ring(sems, at, peer, far_up)

    out_r = [con_ring(con_r, x, x_peer, i, i != 1) for i in range(3)]
    out_c = [con_ring(con_c, z, z_peer, i, i == 1) for i in range(3)]
    for d in (0, 1, 2, 3):
        rings_c[d].last()
    for s in range(SLOTS):
        product = lax.dot_general(gath_c[col_at[s]], tile_buf[s], NT, preferred_element_type=F32) * live[s]
        con_r[x, pl.ds(s * 16, 16), :] = product.astype(BF16)
        if s % 2 == 1:
            out_r[s // 2].first((2, -2))
    for ring in out_r:
        ring.first((1, -1))
    ar0 = group_start(ar0y, yc, y_peer, y_order, group_sum(ar0x, ar0, 8))
    for d in (0, 1, 3, 2):
        rings_r[d].last()
    for s in range(SLOTS):
        product = lax.dot_general(gath_r[row_at[s]], tile_buf[s], NN, preferred_element_type=F32) * live[s]
        con_c[z, pl.ds(s * 16, 16), :] = product.astype(BF16)
        if s % 2 == 1:
            out_c[s // 2].first((2, -2))
    for ring in out_c:
        ring.first((1, -1))
    for ring in out_r + out_c:
        ring.second()
    ar0 = group_start(ar0z, z, z_peer, ring_order, group_sum(ar0y, ar0, 16))
    for c in codes:
        c.wait_recv()

    sub = lax.broadcasted_iota(jnp.int32, (128, 128), 0)

    def reduce_first(buf, code, rings, me_b, me_a, acc, low, part, peer):
        base = (sub + me_b * 128).astype(F32)
        picks = [jnp.where(code[b][0:1, :] == base, 1.0, 0.0).astype(BF16) for b in range(8)]
        for ring in rings:
            ring.last()
        total = jnp.zeros((128, TILE), F32)
        for b in range(0, 8, 2):
            pick = jnp.concatenate(picks[b:b + 2], axis=1)
            total = total + lax.dot_general(
                pick, buf[b:b + 2].reshape(256, TILE), NN, preferred_element_type=F32)
        acc[...] = total.reshape(4, 32, TILE)
        low[...] = total.astype(BF16).reshape(4, 32, TILE)
        return [sems.copy(low.at[(me_a + d) % 4], part.at[d - 1], peer(d)) for d in (2, 1, 3)]

    parts = reduce_first(con_r, code_r, out_r, x, yh, acc_r, low_r, part_r, h_peer)
    parts = parts + reduce_first(con_c, code_c, out_c, z, al, acc_c, low_c, part_c, l_peer)

    pack[...] = jnp.zeros(pack.shape, F32)
    for c in parts:
        c.wait_recv()
    image = acc_r[yh] + acc_c[al]
    for i in range(3):
        image = image + part_r[i].astype(F32) + part_c[i].astype(F32)
    image_cat = jnp.concatenate([image[0:16], image[16:32]], axis=1)
    stack = jnp.concatenate([trial_cat, image_cat, search_cat], axis=0)
    pack[0:16, 0:48] = lax.dot_general(image_cat, stack, NT, precision=HI, preferred_element_type=F32)
    step = group_start(ar1x, x, x_peer, ring_order, pack_rows(pack, 16, 64))

    total = group_sum(ar0z, ar0, 8) / BASIS
    known[0:16] = jnp.concatenate([total, pltpu.roll(total, 96, 1)], axis=0)
    known[16:32] = jnp.concatenate([pltpu.roll(total, 64, 1), pltpu.roll(total, 32, 1)], axis=0)
    row_id = lax.broadcasted_iota(jnp.int32, (16, 128), 0)
    lane_id = lax.broadcasted_iota(jnp.int32, (16, 128), 1)
    ident = jnp.where(lane_id == row_id, 1.0, 0.0).astype(F32)
    work = jnp.where(lane_id < 16, known[0:16], pltpu.roll(ident, 16, 1))
    for j in range(STATES):
        pivot = work[j:j + 1, :] / work[j:j + 1, j:j + 1]
        work = jnp.where(row_id == j, pivot, work - work[:, j:j + 1] * pivot)
    pack[0:16, :] = work
    inverse = pack[0:16, 16:32]
    solved = lax.dot_general(inverse, trial_cat, NN, precision=HI, preferred_element_type=F32)
    side_solved = lax.dot_general(
        inverse, known[0:16, 16:32], NN, precision=HI, preferred_element_type=F32)
    gram[16:32, 16:32] = known[16:32, 16:32]
    sent = len(sems.copies)
    for c in sems.copies:
        c.wait_send()
    step = group_start(ar1y, yc, y_peer, y_order, group_sum(ar1x, step, 8))
    step = group_start(ar1z, z, z_peer, ring_order, group_sum(ar1y, step, 16))
    total = group_sum(ar1z, step, 8) / BASIS

    pack[0:16, :] = jnp.concatenate([total, pltpu.roll(total, 64, 1)], axis=0)
    mixed = pack[0:16, 0:16]
    turned = lax.dot_general(mixed, inverse, NN, precision=HI, preferred_element_type=F32)
    fixed = lax.dot_general(mixed, solved, NN, precision=HI, preferred_element_type=F32)
    residual[0] = image[0:16] - fixed[:, 0:TILE]
    residual[1] = image[16:32] - fixed[:, TILE:]
    rayleigh[...] = lax.dot_general(inverse, mixed, NT, precision=HI, preferred_element_type=F32)
    gram[0:16, 0:16] = pack[0:16, 16:32] - lax.dot_general(
        turned, mixed, NT, precision=HI, preferred_element_type=F32)
    side = pack[0:16, 32:48] - lax.dot_general(
        mixed, side_solved, NN, precision=HI, preferred_element_type=F32)
    gram[0:16, 16:32] = side
    gram[16:32, 0:16] = lax.dot_general(
        ident[:, 0:16], side, NT, precision=HI, preferred_element_type=F32)

    for c in sems.copies[sent:]:
        c.wait_send()


def hand_on(a, b, c, a_out, b_out, c_out):
    a_out[...] = a[...]
    b_out[...] = b[...]
    c_out[...] = c[...]


BASIS = 524288.0
COPIES = 182


def local(tiles, tile_rows, tile_cols, tile_counts, trial, search):
    vmem = pl.BlockSpec(memory_space=pltpu.VMEM)
    results = pl.pallas_call(
        kernel,
        out_shape=(
            pltpu.VMEM((2, STATES, TILE), F32),
            pltpu.VMEM((STATES, STATES), F32),
            pltpu.VMEM((2 * STATES, 2 * STATES), F32),
        ),
        in_specs=[pl.BlockSpec(memory_space=pl.ANY)] * 6,
        out_specs=(vmem, vmem, vmem),
        scratch_shapes=[
            pltpu.VMEM((SLOTS, TILE, TILE), BF16),
            pltpu.VMEM((64, STATES, TILE), BF16),
            pltpu.VMEM((64, STATES, TILE), BF16),
            pltpu.VMEM((8, 128, TILE), BF16),
            pltpu.VMEM((8, 128, TILE), BF16),
            pltpu.VMEM((8, 8, 128), F32),
            pltpu.VMEM((8, 8, 128), F32),
            pltpu.VMEM((4, 32, TILE), F32),
            pltpu.VMEM((4, 32, TILE), F32),
            pltpu.VMEM((4, 32, TILE), BF16),
            pltpu.VMEM((4, 32, TILE), BF16),
            pltpu.VMEM((3, 32, TILE), BF16),
            pltpu.VMEM((3, 32, TILE), BF16),
            pltpu.VMEM((2, STATES, TILE), F32),
            pltpu.VMEM((2, STATES, TILE), F32),
            pltpu.SMEM((1, 1, SLOTS), jnp.int32),
            pltpu.SMEM((1, 1, SLOTS), jnp.int32),
            pltpu.SMEM((1, 1), jnp.int32),
            pltpu.SemaphoreType.DMA((5,)),
        ] + [pltpu.VMEM((n, 8, 128), F32) for n in (8, 16, 8, 8, 16, 8)] + [
            pltpu.VMEM((32, 128), F32),
            pltpu.VMEM((32, 128), F32),
            pltpu.SemaphoreType.DMA,
            pltpu.SemaphoreType.DMA((COPIES,)),
            pltpu.SemaphoreType.DMA((COPIES,)),
        ],
        compiler_params=pltpu.CompilerParams(collective_id=0, has_side_effects=True),
    )(tiles, tile_rows, tile_cols, tile_counts, trial, search)
    return pl.pallas_call(
        hand_on,
        out_shape=tuple(jax.ShapeDtypeStruct(r.shape, F32) for r in results),
        in_specs=[vmem] * 3,
        out_specs=(vmem,) * 3,
    )(*[pltpu.with_memory_space_constraint(r, pltpu.VMEM) for r in results])


def solution(mesh):
    return jax.shard_map(
        local,
        mesh=mesh,
        in_specs=(
            P("row", "col", None, None, None),
            P("row", "col", None),
            P("row", "col", None),
            P("row", "col"),
            P(("row", "col"), None, None),
            P(("row", "col"), None, None),
        ),
        out_specs=(P(("row", "col"), None, None), P(), P()),
        check_vma=False,
    )
```
